128 devices in a mesh: seg: 16 (over z, y_lo, core), section: 8 (over y_hi, x).
Axes of the slice: x: 4, y: 4 (y_hi: 2, y_lo: 2; y = y_hi * 2 + y_lo), z: 4, core: 2. Of those that a mesh axis runs over, the one named last changes fastest.
Arguments:
- leaving: bfloat16 [16, 8, 272, 4096], P('seg', 'section'), may hold values from -6 to 6
- w_query: bfloat16 [8, 4096, 2048], P('section'), may hold values from -0.09375 to 0.09375
- w_key: bfloat16 [8, 4096, 2048], P('section', None, 'seg'), may hold values from -0.09375 to 0.09375
- w_value: bfloat16 [8, 4096, 4096], P('section', None, 'seg'), may hold values from -0.09375 to 0.09375
- w_gate: bfloat16 [8, 4096], P('section'), may hold values from -0.09375 to 0.09375
- norm_gain: bfloat16 [8, 4096], P('section'), may hold values from 0.5 to 1.5
- memory_matrix: bfloat16 [8, 4096, 2048], P('section', 'seg'), may hold values from -24 to 24
- key_totals: float32 [8, 2048], P('section'), may hold values from 0.02 to 0.5
- doc_starts: int32 [8, 16], P('section'), may hold values 0 or 1
Outputs:
- updated: bfloat16 [16, 8, 272, 4096], P('seg', 'section')
- matrix_next: bfloat16 [8, 4096, 2048], P('section', 'seg')
- totals_next: float32 [8, 2048], P('section')
The draws below stay inside these ranges and needn't reach their ends.
All inputs are finite; a program needn't handle non-finite values. No bound on the sum of `doc_starts` on one device may be relied on, other than what follows from the above.
Results may differ from the reference program's by a relative error of at most 0.01.
Values may be sent and summed in bfloat16 or wider, within the bound.
No kernel may reach another device: no remote copies, remote signals or barrier semaphores. Data moves between devices by JAX's collectives and lax.ppermute only.
A program may use at most 128 MiB of HBM per device.

```python
import math
import jax
import jax.numpy as jnp
from jax import lax

D = 4096
DK = 2048
MEM = 16
ROWS = 272
SEGS = 16
SECTIONS = 8


def set_ends(entries, own_key, low, top_value):
    longest = entries.shape.index(max(entries.shape))
    spots = []
    for shift in (0, 1):
        where = [jax.random.randint(jax.random.fold_in(own_key, axis), (), 0, length) for axis, length in enumerate(entries.shape)]
        where[longest] = (where[longest] + shift) % entries.shape[longest]
        spots.append(tuple(where))
    return entries.at[spots[0]].set(low).at[spots[1]].set(top_value)


def block_levels(stream_key, shape, pieces, smallest, top_value):
    def one(position, blocks):
        steps = jax.random.uniform(jax.random.fold_in(jax.random.fold_in(stream_key, 6), position), (blocks,), jnp.float32, smallest / len(pieces), top_value / len(pieces))
        return jnp.repeat(jnp.exp(steps), shape[position] // blocks).reshape((-1,) + (1,) * (len(shape) - position - 1))

    factor_of = one(*pieces[0])
    for cut in pieces[1:]:
        factor_of = factor_of * one(*cut)
    return factor_of


def gaussian(stream_key, shape, width, reach, pieces=(), kind=jnp.bfloat16):
    result = jax.random.normal(stream_key, shape, jnp.float32) * width
    if len(pieces) > 0:
        result = block_levels(stream_key, shape, pieces, -0.22, 0.18) * result
    return jnp.clip(result, min=-reach, max=reach).astype(kind)


def setup_inputs(seed: int = 0) -> dict:
    key_list = jax.random.split(jax.random.key(seed), 10)
    leaving = gaussian(key_list[0], (SEGS, SECTIONS, ROWS, D), 1.0, 6.0, ((0, 16), (1, 8)))
    w_query = gaussian(key_list[1], (SECTIONS, D, DK), D ** -0.5, 0.09375, ((0, 8),))
    w_key = gaussian(key_list[2], (SECTIONS, D, DK), D ** -0.5, 0.09375, ((0, 8), (2, 16)))
    w_value = gaussian(key_list[3], (SECTIONS, D, D), D ** -0.5, 0.09375, ((0, 8), (2, 16)))
    w_gate = gaussian(key_list[4], (SECTIONS, D), D ** -0.5, 0.09375, ((0, 8),))
    norm_gain = jnp.clip(1.0 + 0.1 * jax.random.normal(key_list[5], (SECTIONS, D), jnp.float32), 0.5, 1.5).astype(jnp.bfloat16)
    memory_matrix = gaussian(key_list[6], (SECTIONS, D, DK), 4.0, 24.0, ((0, 8), (1, 16)))
    key_totals = jnp.clip(jnp.exp(math.log(0.5) - 3.218876 * jax.random.uniform(key_list[7], (SECTIONS, DK), jnp.float32) ** block_levels(key_list[7], (SECTIONS, DK), ((0, 8),), -0.2, 0.2)), 0.02, 0.5)
    doc_starts = set_ends((jax.random.randint(key_list[8], (SECTIONS, SEGS), 0, 8) < 1).astype(jnp.int32), jax.random.fold_in(key_list[8], 1), 0, 1)
    return {"leaving": leaving, "w_query": w_query, "w_key": w_key, "w_value": w_value, "w_gate": w_gate, "norm_gain": norm_gain, "memory_matrix": memory_matrix, "key_totals": key_totals, "doc_starts": doc_starts}


highest = lax.Precision.HIGHEST
epsilon = 1e-05

def feature_map(projected):
    return jax.nn.elu(projected) + 1.0

def visibility(starts_row):
    seg_total = starts_row.shape[0]
    positions = jnp.arange(seg_total, dtype=jnp.int32)
    last_start = lax.cummax(jnp.where(starts_row == 1, positions, jnp.int32(-1)), axis=0)
    fresh_flag = (last_start < 0).astype(jnp.float32)
    seen_pairs = ((positions[:, None] >= last_start[None, :]) & (positions[:, None] < positions[None, :])).astype(jnp.float32)
    seen_final = (positions >= last_start[seg_total - 1]).astype(jnp.float32)
    return (fresh_flag, seen_pairs, seen_final)

def one_section(entering, query_proj, key_proj, value_proj, gate_vector, gain_row, matrix, totals_base, starts_row):
    seg_count = entering.shape[0]
    row_count = entering.shape[1]
    feature_count = entering.shape[2]
    wide_rows = entering.astype(jnp.float32)
    inverse_rms = lax.rsqrt(lax.optimization_barrier(jnp.mean(wide_rows * wide_rows, axis=-1, keepdims=True)) + epsilon)
    normed = (wide_rows * inverse_rms * gain_row.astype(jnp.float32)).astype(jnp.bfloat16)
    flat_rows = normed.reshape(seg_count * row_count, feature_count)
    queries = feature_map(jnp.dot(flat_rows, query_proj, preferred_element_type=jnp.float32)).astype(jnp.bfloat16)
    memory = normed[:, :MEM, :].reshape(seg_count * MEM, feature_count)
    key_rows = feature_map(jnp.dot(memory, key_proj, preferred_element_type=jnp.float32)).astype(jnp.bfloat16)
    values = jnp.dot(memory, value_proj, preferred_element_type=jnp.float32)
    gate_rates = jax.nn.sigmoid(jnp.dot(memory, gate_vector, preferred_element_type=jnp.float32))
    fresh_flag, seen_pairs, seen_final = visibility(starts_row)
    key_wide = key_rows.astype(jnp.float32)
    key_sums = key_wide.reshape(seg_count, MEM, -1).sum(axis=1)
    totals = fresh_flag[:, None] * totals_base[None, :] + jnp.dot(seen_pairs.T, key_sums, precision=highest)
    total_rows = jnp.repeat(totals, MEM, axis=0)
    key_scales = jnp.maximum(lax.optimization_barrier(jnp.sum(total_rows * key_wide, axis=-1)), 1.0)
    fresh_rows = jnp.repeat(fresh_flag, MEM)
    key_gram = jnp.dot(key_rows, key_rows.T, preferred_element_type=jnp.float32)
    probed_keys = jnp.dot(key_rows, matrix.T, preferred_element_type=jnp.float32)
    initial = gate_rates[:, None] * (values - fresh_rows[:, None] * probed_keys / key_scales[:, None])
    seen_cols = jnp.repeat(jnp.repeat(seen_pairs, MEM, axis=0), MEM, axis=1)
    mixing = seen_cols * key_gram * (gate_rates / key_scales)[None, :]
    writes = jnp.zeros_like(values)
    for segment in range(seg_count):
        mix_cols = mixing[:, segment * MEM:(segment + 1) * MEM]
        candidate = initial[segment * MEM:(segment + 1) * MEM] - jnp.dot(mix_cols.T, writes, precision=highest)
        writes = writes.at[segment * MEM:(segment + 1) * MEM].set(candidate)
    base_read = jnp.dot(queries, matrix.T, preferred_element_type=jnp.float32)
    column_mask = jnp.repeat(jnp.repeat(seen_pairs.T, row_count, axis=0), MEM, axis=1)
    similarity = jnp.dot(queries, key_rows.T, preferred_element_type=jnp.float32) * column_mask
    low_rank = jnp.dot(similarity, writes, precision=highest)
    query_totals = jnp.repeat(totals, row_count, axis=0)
    denominator = jnp.maximum(lax.optimization_barrier(jnp.sum(queries.astype(jnp.float32) * query_totals, axis=-1)), 1.0)
    fresh_query = jnp.repeat(fresh_flag, row_count)
    updated = (wide_rows.reshape(seg_count * row_count, feature_count) + (fresh_query[:, None] * base_read + low_rank) / denominator[:, None]).astype(jnp.bfloat16)
    updated = updated.reshape(seg_count, row_count, feature_count)
    fresh_end = fresh_flag[seg_count - 1]
    end_rows = jnp.repeat(seen_final, MEM)
    matrix_next = (fresh_end * matrix.astype(jnp.float32) + jnp.dot((writes * end_rows[:, None]).T, key_wide, precision=highest)).astype(jnp.bfloat16)
    totals_next = fresh_end * totals_base + jnp.dot(seen_final, key_sums, precision=highest)
    return (updated, matrix_next, totals_next)

def reference(leaving, w_query, w_key, w_value, w_gate, norm_gain, memory_matrix, key_totals, doc_starts):
    entering = jnp.moveaxis(jnp.roll(leaving, 1, axis=1), 1, 0)

    def section_work(packed):
        return one_section(*packed)
    updated, matrix_next, totals_next = lax.map(section_work, (entering, w_query, w_key, w_value, w_gate, norm_gain, memory_matrix, key_totals, doc_starts))
    return (jnp.moveaxis(updated, 0, 1), matrix_next, totals_next)
```

```python
import jax
import jax.numpy as jnp
from jax import lax
from jax.experimental import pallas as pl
from jax.experimental.pallas import tpu as pltpu
from jax.sharding import PartitionSpec as P

MEM = 16
EPS = 1e-05
INTERPRET = False
F32 = jnp.float32
BF16 = jnp.bfloat16


VM = pl.BlockSpec(memory_space=pltpu.VMEM)
SM = pl.BlockSpec(memory_space=pltpu.SMEM)


def permute(block, axis, target):
    size = lax.axis_size(axis)
    return lax.ppermute(block, axis, [(i, target(i)) for i in range(size)])


def shifted(block):
    return permute(block, "section", lambda i: (i + 1) % lax.axis_size("section"))


def offsets():
    half = [(0, 0), (0, 1), (3, 0), (1, 0), (2, 0), (2, 1), (3, 1), (1, 1)]
    return [(dz, dy, dc) for dc in (0, 1) for dz, dy in half]


def gather_slots(block):
    across = permute(block, "seg", lambda i: i ^ 2)
    below = permute(block, "seg", lambda i: (i + 4) % 16)
    above = permute(block, "seg", lambda i: (i - 4) % 16)
    far = permute(jnp.stack([block, across]), "seg", lambda i: i ^ 8)
    diagonal = permute(jnp.stack([below, above]), "seg", lambda i: i ^ 2)
    mine = jnp.concatenate(
        [jnp.stack([block, across, below, above]), far, diagonal], axis=0
    )
    return jnp.stack([mine, permute(mine, "seg", lambda i: i ^ 1)]).reshape(
        (16,) + block.shape
    )


def slot_segments(me):
    z, y, c = me // 4, (me // 2) % 2, me % 2
    dz, dy, dc = (jnp.array(v, jnp.int32) for v in zip(*offsets()))
    return ((z + dz) % 4) * 4 + (y ^ dy) * 2 + (c ^ dc)


def split(x):
    high = x.astype(BF16)
    return high, (x - high.astype(F32)).astype(BF16)


def dot(a, b, contract=((1,), (0,))):
    return lax.dot_general(a, b, (contract, ((), ())), preferred_element_type=F32)


def dot3(a, b):
    ah, al = a
    bh, bl = b
    return dot(ah, bh) + (dot(ah, bl) + dot(al, bh))


def phi(x):
    return jnp.where(x > 0, x, jnp.exp(jnp.minimum(x, 0.0)) - 1.0) + 1.0


def normalise(rows, gain):
    wide = rows.astype(F32)
    inverse = lax.rsqrt(jnp.mean(wide * wide, axis=-1, keepdims=True) + EPS)
    return (wide * inverse * gain.astype(F32)).astype(BF16)


def last_starts(starts_ref, count):
    lasts, last = [], jnp.int32(-1)
    for s in range(count):
        last = jnp.where(starts_ref[0, s] == 1, jnp.int32(s), last)
        lasts.append(last)
    return lasts


def norm_kernel(rows_ref, gain_ref, out_ref):
    out_ref[...] = normalise(rows_ref[...], gain_ref[...])


def kv_kernel(slots_ref, memory_ref, key_ref, value_ref, gate_ref, key_out, value_out, gate_out):
    count = memory_ref.shape[0]
    memory = memory_ref[...].reshape(count * MEM, memory_ref.shape[2])
    keys = phi(dot(memory, key_ref[...])).astype(BF16)
    values = dot(memory, value_ref[...])
    gate = jnp.broadcast_to(gate_ref[...], (8, gate_ref.shape[1]))
    rates = jax.nn.sigmoid(dot(memory, gate, ((1,), (1,))))[:, :1]
    rates = jnp.broadcast_to(rates, (count * MEM, 128))
    for slot in range(count):
        rows = pl.ds(pl.multiple_of(slots_ref[slot] * MEM, MEM), MEM)
        part = slice(slot * MEM, (slot + 1) * MEM)
        key_out[rows, :] = keys[part]
        value_out[rows, :] = values[part]
        gate_out[rows, :] = rates[part]


def solve_kernel(slots_ref, starts_ref, pieces_ref, values_ref, rates_ref, matrix_ref, totals_ref, keys_out, writes_out):
    count, rows, width = pieces_ref.shape
    for slot in range(count):
        cols = pl.ds(pl.multiple_of(slots_ref[slot] * width, width), width)
        keys_out[:, cols] = pieces_ref[slot]
    keys = keys_out[...]
    gram = dot(keys, keys, ((1,), (1,)))
    probed = dot(keys, matrix_ref[...], ((1,), (1,)))
    own = lax.broadcasted_iota(jnp.int32, (rows, 1), 0) // MEM
    other = lax.broadcasted_iota(jnp.int32, (rows, rows), 1) // MEM
    last = jnp.full((rows, 1), -1, jnp.int32)
    for s, value in enumerate(last_starts(starts_ref, count)):
        last = jnp.where(own == s, value, last)
    fresh = (last < 0).astype(F32)
    masked = jnp.where((other >= last) & (other < own), gram, 0.0)
    base = jnp.sum(keys.astype(F32) * totals_ref[...], axis=-1, keepdims=True)
    scales = jnp.maximum(fresh * base + jnp.sum(masked, axis=-1, keepdims=True), 1.0)
    rates = rates_ref[:, :1]
    current = rates * (values_ref[...] - fresh * probed / scales)
    power = split(masked * (rates / scales))
    current = current - dot3(power, split(current))
    for step in range(3):
        power = split(dot3(power, power))
        current = current + dot3(power, split(current))
    writes_out[...] = current


def next_kernel(starts_ref, keys_ref, writes_ref, matrix_ref, totals_ref, matrix_out, totals_out):
    rows = keys_ref.shape[0]
    last = last_starts(starts_ref, rows // MEM)[-1]
    fresh = (last < 0).astype(F32)
    keys = keys_ref[...]
    own = lax.broadcasted_iota(jnp.int32, (rows, 1), 0) // MEM
    writes = jnp.where(own >= last, writes_ref[...], 0.0)
    high, low = split(writes)
    added = dot(high, keys, ((0,), (0,))) + dot(low, keys, ((0,), (0,)))
    matrix_out[...] = (fresh * matrix_ref[...].astype(F32) + added).astype(BF16)
    seen = lax.broadcasted_iota(jnp.int32, (8, rows), 1) // MEM >= last
    sums = dot(seen.astype(F32).astype(BF16), keys)[:1]
    totals_out[...] = fresh * totals_ref[...] + sums


def query_kernel(rows_ref, gain_ref, weight_ref, out_ref, normed_ref):
    @pl.when(pl.program_id(0) == 0)
    def _():
        normed_ref[...] = normalise(rows_ref[...], gain_ref[...])

    out_ref[...] = phi(dot(normed_ref[...], weight_ref[...])).astype(BF16)


def similarity_kernel(me_ref, starts_ref, queries_ref, keys_ref, totals_ref, high_out, low_out, inverse_out):
    rows = keys_ref.shape[0]
    me = me_ref[0]
    last = jnp.int32(-1)
    for s, value in enumerate(last_starts(starts_ref, rows // MEM)):
        last = jnp.where(me == s, value, last)
    fresh = (last < 0).astype(F32)
    queries = queries_ref[...]
    other = lax.broadcasted_iota(jnp.int32, (1, rows), 1) // MEM
    masked = jnp.where((other >= last) & (other < me), dot(queries, keys_ref[...], ((1,), (1,))), 0.0)
    base = jnp.sum(queries.astype(F32) * totals_ref[...], axis=-1, keepdims=True)
    inverse = 1.0 / jnp.maximum(fresh * base + jnp.sum(masked, axis=-1, keepdims=True), 1.0)
    high_out[...], low_out[...] = split(masked)
    lane = lax.broadcasted_iota(jnp.int32, inverse_out.shape, 1)
    inverse_out[...] = jnp.where(lane < 64, inverse, inverse * fresh)


def read_kernel(slot_of_ref, queries_ref, high_ref, low_ref, inverse_ref, rows_ref, matrix_ref, writes_ref, out_ref):
    base = dot(queries_ref[...], matrix_ref[...], ((1,), (1,)))
    writes = writes_ref[0]
    low = dot(high_ref[...], writes) + dot(low_ref[...], writes)
    inverse = inverse_ref[:, :1]
    fresh = inverse_ref[:, 64:65]
    out_ref[...] = (rows_ref[...].astype(F32) + (fresh * base + inverse * low)).astype(BF16)


def call(kernel, outs, *args, specs, scratch=()):
    return pl.pallas_call(
        kernel, out_shape=outs, in_specs=list(specs),
        out_specs=jax.tree.map(lambda _: VM, outs), scratch_shapes=scratch, interpret=INTERPRET,
    )(*args)


def shape(dims, kind):
    return jax.ShapeDtypeStruct(dims, kind)


def local(leaving, w_query, w_key, w_value, w_gate, norm_gain, memory_matrix, key_totals, doc_starts):
    me = lax.axis_index("seg").astype(jnp.int32)
    slots = slot_segments(me)
    slot_of = jnp.zeros((16,), jnp.int32).at[slots].set(jnp.arange(16, dtype=jnp.int32))
    mine = jnp.full((1,), me)
    leaving, matrix = leaving[0, 0], memory_matrix[0]
    width, features, depth = matrix.shape[0], leaving.shape[1], matrix.shape[1]
    head = shifted(leaving[:MEM])
    tail = shifted(leaving[MEM:])
    whole = lax.all_gather(matrix, "seg", axis=0, tiled=True)

    normed = call(norm_kernel, shape((MEM, features), BF16), head, norm_gain, specs=[VM, VM])
    memory = gather_slots(normed)
    rows = 16 * MEM
    key_part, values, rates = call(
        kv_kernel,
        (shape((rows, w_key.shape[2]), BF16), shape((rows, width), F32), shape((rows, 128), F32)),
        slots, memory, w_key[0], w_value[0], w_gate,
        specs=[SM, VM, VM, VM, VM],
    )
    pieces = gather_slots(key_part)
    keys, writes = call(
        solve_kernel,
        (shape((rows, depth), BF16), shape((rows, width), F32)),
        slots, doc_starts, pieces, values, rates, matrix, key_totals,
        specs=[SM, SM, VM, VM, VM, VM, VM],
    )
    write_slots = gather_slots(writes.astype(BF16))
    matrix_next, totals_next = call(
        next_kernel,
        (shape((width, depth), BF16), shape((1, depth), F32)),
        doc_starts, keys, writes, matrix, key_totals,
        specs=[SM, VM, VM, VM, VM],
    )

    entering = jnp.concatenate([head, tail], axis=0)
    count = entering.shape[0]
    block = depth // 8
    queries = pl.pallas_call(
        query_kernel,
        out_shape=shape((count, depth), BF16),
        grid=(8,),
        in_specs=[
            pl.BlockSpec((count, features), lambda j: (0, 0)),
            pl.BlockSpec((1, features), lambda j: (0, 0)),
            pl.BlockSpec((features, block), lambda j: (0, j)),
        ],
        out_specs=pl.BlockSpec((count, block), lambda j: (0, j)),
        scratch_shapes=[pltpu.VMEM((count, features), BF16)],
        interpret=INTERPRET,
    )(entering, norm_gain, w_query[0])
    high, low, inverse = call(
        similarity_kernel,
        (shape((count, rows), BF16), shape((count, rows), BF16), shape((count, 128), F32)),
        mine, doc_starts, queries, keys, key_totals,
        specs=[SM, SM, VM, VM, VM],
    )
    updated = pl.pallas_call(
        read_kernel,
        out_shape=shape((count, features), BF16),
        grid_spec=pltpu.PrefetchScalarGridSpec(
            num_scalar_prefetch=1,
            grid=(16,),
            in_specs=[
                pl.BlockSpec((count, depth), lambda j, s: (0, 0)),
                pl.BlockSpec((count, rows), lambda j, s: (0, 0)),
                pl.BlockSpec((count, rows), lambda j, s: (0, 0)),
                pl.BlockSpec((count, 128), lambda j, s: (0, 0)),
                pl.BlockSpec((count, width), lambda j, s: (0, j)),
                pl.BlockSpec((width, depth), lambda j, s: (j, 0)),
                pl.BlockSpec((1, rows, width), lambda j, s: (s[j], 0, 0)),
            ],
            out_specs=pl.BlockSpec((count, width), lambda j, s: (0, j)),
        ),
        interpret=INTERPRET,
    )(slot_of, queries, high, low, inverse, entering, whole, write_slots)
    return updated[None, None], matrix_next[None], totals_next


def solution(mesh):
    return jax.shard_map(
        local,
        mesh=mesh,
        in_specs=(
            P("seg", "section", None, None),
            P("section", None, None),
            P("section", None, "seg"),
            P("section", None, "seg"),
            P("section", None),
            P("section", None),
            P("section", "seg", None),
            P("section", None),
            P("section", None),
        ),
        out_specs=(P("seg", "section", None, None), P("section", "seg", None), P("section", None)),
        check_vma=False,
    )
```

```python
import jax
import jax.numpy as jnp
from jax import lax
from jax.experimental import pallas as pl
from jax.experimental.pallas import tpu as pltpu
from jax.sharding import PartitionSpec as P


MEM = 16
EPS = 1e-05
INTERPRET = False
F32 = jnp.float32
BF16 = jnp.bfloat16


VM = pl.BlockSpec(memory_space=pltpu.VMEM)
SM = pl.BlockSpec(memory_space=pltpu.SMEM)


def permute(block, axis, target):
    size = lax.axis_size(axis)
    return lax.ppermute(block, axis, [(i, target(i)) for i in range(size)])


def shifted(block):
    return permute(block, "section", lambda i: (i + 1) % lax.axis_size("section"))


def shifted_across(block):
    wide = lax.axis_size("section")
    pairs = [
        (s * wide + p, (s ^ 2) * wide + (p + 1) % wide)
        for s in range(lax.axis_size("seg"))
        for p in range(wide)
    ]
    return lax.ppermute(block, ("seg", "section"), pairs)


def shifted_rows(block):
    wide, run = lax.axis_size("section"), lax.axis_size("section") // 2
    ends = [p for p in range(wide) if p % run == run - 1]
    segs = range(lax.axis_size("seg"))
    late = [s for s in segs if (s ^ (s // 2)) % 2]

    def send(part, pairs):
        return lax.ppermute(part, ("seg", "section"), [(s * wide + p, s * wide + q) for s, p, q in pairs])

    plain = send(block, [(s, p, p + 1) for s in segs for p in range(wide) if p not in ends])
    first = send(block, [(s, p, (p + 1) % wide) for s in segs if s not in late for p in ends])
    second = send(block, [(s, p, (p + run) % wide) for s in late for p in ends])
    second = send(second, [(s, p, p + 1 - run) for s in late for p in ends])
    source = jnp.where(
        lax.axis_index("section") % run > 0, 0,
        jnp.where(jnp.isin(lax.axis_index("seg"), jnp.array(late)), 2, 1),
    )
    return source.astype(jnp.int32)[None], plain, first, second


def offsets():
    return [(dz, dy, dc) for dc in (0, 1) for dy in (0, 1) for dz in (0, 3, 1, 2)]


def gather_slots(block):
    def send(part, target):
        return permute(part, "seg", target)

    below = send(block, lambda i: (i + 4) % 16)
    above = send(block, lambda i: (i - 4) % 16)
    far = send(block, lambda i: i ^ 8)
    near = jnp.stack([block, below, above, far])
    across = send(near, lambda i: i ^ 2)
    return near, across, send(near, lambda i: i ^ 1), send(across, lambda i: i ^ 1)


def gather_pairs(block):
    def send(part, target):
        return permute(part, "seg", target)

    below = send(block, lambda i: (i + 4) % 16)
    above = send(block, lambda i: (i - 4) % 16)
    far = send(block, lambda i: i ^ 8)
    mine = (block, below, above, far)
    return mine + tuple(send(part, lambda i: i ^ 1) for part in mine)


def pair_offsets():
    return [(dz, dy, dc) for dc in (0, 1) for dz in (0, 3, 1, 2) for dy in (0, 1)]


def slot_segments(me, order):
    z, y, c = me // 4, (me // 2) % 2, me % 2
    dz, dy, dc = (jnp.array(v, jnp.int32) for v in zip(*order))
    return ((z + dz) % 4) * 4 + (y ^ dy) * 2 + (c ^ dc)


def split(x):
    high = x.astype(BF16)
    return high, (x - high.astype(F32)).astype(BF16)


def dot(a, b, contract=((1,), (0,))):
    return lax.dot_general(a, b, (contract, ((), ())), preferred_element_type=F32)


def dot3(a, b):
    ah, al = a
    bh, bl = b
    return dot(ah, bh) + (dot(ah, bl) + dot(al, bh))


def phi(x):
    return jnp.where(x > 0, x, jnp.exp(jnp.minimum(x, 0.0)) - 1.0) + 1.0


def normalise(rows, gain):
    wide = rows.astype(F32)
    inverse = lax.rsqrt(jnp.mean(wide * wide, axis=-1, keepdims=True) + EPS)
    return (wide * inverse * gain.astype(F32)).astype(BF16)


def last_starts(starts_ref, count):
    lasts, last = [], jnp.int32(-1)
    for s in range(count):
        last = jnp.where(starts_ref[0, s] == 1, jnp.int32(s), last)
        lasts.append(last)
    return lasts


def norm_kernel(rows_ref, across_ref, gain_ref, out_ref):
    out_ref[0] = normalise(rows_ref[...], gain_ref[...])
    out_ref[1] = normalise(across_ref[...], gain_ref[...])


def kv_kernel(slots_ref, *refs):
    pairs, (key_ref, value_ref, gate_ref, key_out, value_out, gate_out) = refs[:8], refs[8:]
    count = 16
    memory = jnp.concatenate([ref[...] for ref in pairs], axis=0)
    memory = memory.reshape(count * MEM, memory.shape[2])
    keys = phi(dot(memory, key_ref[...])).astype(BF16)
    values = dot(memory, value_ref[...])
    gate = jnp.broadcast_to(gate_ref[...], (8, gate_ref.shape[1]))
    rates = jax.nn.sigmoid(dot(memory, gate, ((1,), (1,))))[:, :1]
    rates = jnp.broadcast_to(rates, (count * MEM, 128))
    for slot in range(count):
        rows = pl.ds(pl.multiple_of(slots_ref[slot] * MEM, MEM), MEM)
        part = slice(slot * MEM, (slot + 1) * MEM)
        key_out[rows, :] = keys[part]
        value_out[rows, :] = values[part]
        gate_out[rows, :] = rates[part]


def solve_kernel(slots_ref, starts_ref, a_ref, b_ref, c_ref, d_ref, values_ref, rates_ref, matrix_ref, totals_ref, keys_out, writes_out, sent_out):
    pieces = (a_ref, b_ref, c_ref, d_ref)
    each, rows, width = a_ref.shape
    count = 4 * each
    for slot in range(count):
        cols = pl.ds(pl.multiple_of(slots_ref[slot] * width, width), width)
        keys_out[:, cols] = pieces[slot // each][slot % each]
    keys = keys_out[...]
    gram = dot(keys, keys, ((1,), (1,)))
    probed = dot(keys, matrix_ref[...], ((1,), (1,)))
    own = lax.broadcasted_iota(jnp.int32, (rows, 1), 0) // MEM
    other = lax.broadcasted_iota(jnp.int32, (rows, rows), 1) // MEM
    last = jnp.full((rows, 1), -1, jnp.int32)
    for s, value in enumerate(last_starts(starts_ref, count)):
        last = jnp.where(own == s, value, last)
    fresh = (last < 0).astype(F32)
    masked = jnp.where((other >= last) & (other < own), gram, 0.0)
    base = jnp.sum(keys.astype(F32) * totals_ref[...], axis=-1, keepdims=True)
    scales = jnp.maximum(fresh * base + jnp.sum(masked, axis=-1, keepdims=True), 1.0)
    rates = rates_ref[:, :1]
    current = rates * (values_ref[...] - fresh * probed / scales)
    power = split(masked * (rates / scales))
    current = current - dot3(power, split(current))
    for _ in range(3):
        power = split(dot3(power, power))
        current = current + dot3(power, split(current))
    writes_out[...] = current
    sent_out[...] = current.astype(BF16)


def next_kernel(starts_ref, keys_ref, writes_ref, matrix_ref, totals_ref, matrix_out, totals_out):
    rows = keys_ref.shape[0]
    last = last_starts(starts_ref, rows // MEM)[-1]
    fresh = (last < 0).astype(F32)
    keys = keys_ref[...]
    own = lax.broadcasted_iota(jnp.int32, (rows, 1), 0) // MEM
    writes = jnp.where(own >= last, writes_ref[...], 0.0)
    high, low = split(writes)
    added = dot(high, keys, ((0,), (0,))) + dot(low, keys, ((0,), (0,)))
    matrix_out[...] = (fresh * matrix_ref[...].astype(F32) + added).astype(BF16)
    seen = lax.broadcasted_iota(jnp.int32, (8, rows), 1) // MEM >= last
    sums = dot(seen.astype(F32).astype(BF16), keys)[:1]
    totals_out[...] = fresh * totals_ref[...] + sums


def query_kernel(source_ref, first_ref, second_ref, third_ref, gain_ref, weight_ref, out_ref, rows_ref, normed_ref, arrived):
    @pl.when(pl.program_id(0) == 0)
    def _():
        for number, ref in enumerate((first_ref, second_ref, third_ref)):

            @pl.when(source_ref[0] == number)
            def _(ref=ref):
                copy = pltpu.make_async_copy(ref, rows_ref, arrived)
                copy.start()
                copy.wait()

        normed_ref[...] = normalise(rows_ref[...], gain_ref[...])

    out_ref[...] = phi(dot(normed_ref[...], weight_ref[...])).astype(BF16)


def similarity_kernel(me_ref, starts_ref, queries_ref, keys_ref, totals_ref, high_out, low_out, inverse_out):
    rows = keys_ref.shape[0]
    me = me_ref[0]
    last = jnp.int32(-1)
    for s, value in enumerate(last_starts(starts_ref, rows // MEM)):
        last = jnp.where(me == s, value, last)
    fresh = (last < 0).astype(F32)
    queries = queries_ref[...]
    other = lax.broadcasted_iota(jnp.int32, (1, rows), 1) // MEM
    masked = jnp.where((other >= last) & (other < me), dot(queries, keys_ref[...], ((1,), (1,))), 0.0)
    base = jnp.sum(queries.astype(F32) * totals_ref[...], axis=-1, keepdims=True)
    inverse = 1.0 / jnp.maximum(fresh * base + jnp.sum(masked, axis=-1, keepdims=True), 1.0)
    high_out[...], low_out[...] = split(masked)
    lane = lax.broadcasted_iota(jnp.int32, inverse_out.shape, 1)
    inverse_out[...] = jnp.where(lane < 64, inverse, inverse * fresh)


def read_kernel(place_ref, queries_ref, high_ref, low_ref, inverse_ref, rows_ref, matrix_ref, mine_ref, theirs_ref, *rest):
    out_ref = rest[-1]
    width = mine_ref.shape[2]
    base = dot(queries_ref[...], matrix_ref[...], ((1,), (1,)))
    inverse = inverse_ref[:, :1]
    fresh = inverse_ref[:, 64:65]
    swap = place_ref[1] == 1
    for side in range(2):
        cols = slice(side * width, (side + 1) * width)
        writes = jnp.where(swap == (side == 0), theirs_ref[0], mine_ref[0])
        low = dot(high_ref[...], writes) + dot(low_ref[...], writes)
        out_ref[:, cols] = (rows_ref[:, cols].astype(F32) + (fresh * base[:, cols] + inverse * low)).astype(BF16)


def read_half(half, me, queries, high, low, inverse, entering, matrix, writes, previous=None):
    count, depth = queries.shape
    rows, width = writes[0].shape[1:]
    distance = (jnp.arange(4, dtype=jnp.int32) - me // 4) % 4
    slot_of = jnp.where(distance == 3, 1, jnp.where(distance == 0, 0, distance + 1))
    place = jnp.concatenate([jnp.stack([half, me % 2]), slot_of])
    args = [place, queries, high, low, inverse, entering, matrix, *writes]
    specs = [
        pl.BlockSpec((count, depth), lambda z, p: (0, 0)),
        pl.BlockSpec((count, rows), lambda z, p: (0, 0)),
        pl.BlockSpec((count, rows), lambda z, p: (0, 0)),
        pl.BlockSpec((count, 128), lambda z, p: (0, 0)),
        pl.BlockSpec((count, 2 * width), lambda z, p: (0, 2 * z + p[0])),
        pl.BlockSpec((2 * width, depth), lambda z, p: (z, 0)),
        pl.BlockSpec((1, rows, width), lambda z, p: (p[2 + z], 0, 0)),
        pl.BlockSpec((1, rows, width), lambda z, p: (p[2 + z], 0, 0)),
    ]
    if previous is not None:
        args.append(previous)
        specs.append(pl.BlockSpec(memory_space=pl.ANY))
    return pl.pallas_call(
        read_kernel,
        out_shape=shape(entering.shape, BF16),
        grid_spec=pltpu.PrefetchScalarGridSpec(
            num_scalar_prefetch=1,
            grid=(4,),
            in_specs=specs,
            out_specs=pl.BlockSpec((count, 2 * width), lambda z, p: (0, 2 * z + p[0])),
        ),
        input_output_aliases={} if previous is None else {len(args) - 1: 0},
        interpret=INTERPRET,
    )(*args)


def call(kernel, outs, *args, specs, scratch=()):
    return pl.pallas_call(
        kernel, out_shape=outs, in_specs=list(specs),
        out_specs=jax.tree.map(lambda _: VM, outs), scratch_shapes=scratch, interpret=INTERPRET,
    )(*args)


def shape(dims, kind):
    return jax.ShapeDtypeStruct(dims, kind)


def local(leaving, w_query, w_key, w_value, w_gate, norm_gain, memory_matrix, key_totals, doc_starts):
    me = lax.axis_index("seg").astype(jnp.int32)
    slots = slot_segments(me, offsets())
    pair_slots = slot_segments(me, pair_offsets())
    mine = jnp.full((1,), me)
    leaving, matrix = leaving[0, 0], memory_matrix[0]
    width, features, depth = matrix.shape[0], leaving.shape[1], matrix.shape[1]
    rows = 16 * MEM
    head = shifted(leaving[:MEM])
    across = shifted_across(leaving[:MEM])
    entering = shifted_rows(leaving)
    groups = [[i for i in range(16) if (i // 2) % 2 == y] for y in (0, 1)]
    near = lax.all_gather(matrix, "seg", axis=0, tiled=True, axis_index_groups=groups)
    partner = permute(matrix, "seg", lambda i: i ^ 2)
    away = lax.all_gather(partner, "seg", axis=0, tiled=True, axis_index_groups=groups)

    normed = call(
        norm_kernel, shape((2, MEM, features), BF16), head, across, norm_gain, specs=[VM] * 3
    )
    memory = gather_pairs(normed)
    key_part, values, rates = call(
        kv_kernel,
        (shape((rows, w_key.shape[2]), BF16), shape((rows, width), F32), shape((rows, 128), F32)),
        pair_slots, *memory, w_key[0], w_value[0], w_gate,
        specs=[SM] + [VM] * 11,
    )
    pieces = gather_slots(key_part)
    keys, writes, sent = call(
        solve_kernel,
        (shape((rows, depth), BF16), shape((rows, width), F32), shape((rows, width), BF16)),
        slots, doc_starts, *pieces, values, rates, matrix, key_totals,
        specs=[SM, SM] + [VM] * 8,
    )
    write_slots = gather_slots(sent)
    matrix_next, totals_next = call(
        next_kernel,
        (shape((width, depth), BF16), shape((1, depth), F32)),
        doc_starts, keys, writes, matrix, key_totals,
        specs=[SM] + [VM] * 4,
    )

    count = leaving.shape[0]
    block = depth // 4
    queries, entering = pl.pallas_call(
        query_kernel,
        out_shape=(shape((count, depth), BF16), shape((count, features), BF16)),
        grid=(4,),
        in_specs=[
            SM,
            pl.BlockSpec(memory_space=pl.ANY),
            pl.BlockSpec(memory_space=pl.ANY),
            pl.BlockSpec(memory_space=pl.ANY),
            pl.BlockSpec((1, features), lambda j: (0, 0)),
            pl.BlockSpec((features, block), lambda j: (0, j)),
        ],
        out_specs=(pl.BlockSpec((count, block), lambda j: (0, j)), pl.BlockSpec((count, features), lambda j: (0, 0))),
        scratch_shapes=[pltpu.VMEM((count, features), BF16), pltpu.SemaphoreType.DMA],
        interpret=INTERPRET,
    )(*entering, norm_gain, w_query[0])
    high, low, inverse = call(
        similarity_kernel,
        (shape((count, rows), BF16), shape((count, rows), BF16), shape((count, 128), F32)),
        mine, doc_starts, queries, keys, key_totals,
        specs=[SM, SM] + [VM] * 3,
    )
    half = (me // 2) % 2
    parts = (me, queries, high, low, inverse, entering)
    updated = read_half(half, *parts, near, write_slots[0::2])
    updated = read_half(1 - half, *parts, away, write_slots[1::2], updated)
    return updated[None, None], matrix_next[None], totals_next


def solution(mesh):
    return jax.shard_map(
        local,
        mesh=mesh,
        in_specs=(
            P("seg", "section", None, None),
            P("section", None, None),
            P("section", None, "seg"),
            P("section", None, "seg"),
            P("section", None),
            P("section", None),
            P("section", "seg", None),
            P("section", None),
            P("section", None),
        ),
        out_specs=(P("seg", "section", None, None), P("section", "seg", None), P("section", None)),
        check_vma=False,
    )
```

```python
import functools

import jax
import jax.numpy as jnp
from jax import lax
from jax.experimental import pallas as pl
from jax.experimental.pallas import tpu as pltpu
from jax.sharding import PartitionSpec as P


MEM = 16
EPS = 1e-05
INTERPRET = False
F32 = jnp.float32
BF16 = jnp.bfloat16


VM = pl.BlockSpec(memory_space=pltpu.VMEM)
SM = pl.BlockSpec(memory_space=pltpu.SMEM)


def permute(block, axis, target):
    size = lax.axis_size(axis)
    return lax.ppermute(block, axis, [(i, target(i)) for i in range(size)])


def shifted(block):
    return permute(block, "section", lambda i: (i + 1) % lax.axis_size("section"))


def shifted_across(block):
    wide = lax.axis_size("section")
    pairs = [
        (s * wide + p, (s ^ 2) * wide + (p + 1) % wide)
        for s in range(lax.axis_size("seg"))
        for p in range(wide)
    ]
    return lax.ppermute(block, ("seg", "section"), pairs)


def shifted_rows(block):
    wide, run = lax.axis_size("section"), lax.axis_size("section") // 2
    ends = [p for p in range(wide) if p % run == run - 1]
    segs = range(lax.axis_size("seg"))
    late = [s for s in segs if (s ^ (s // 2)) % 2]

    def send(part, pairs):
        return lax.ppermute(part, ("seg", "section"), [(s * wide + p, s * wide + q) for s, p, q in pairs])

    plain = send(block, [(s, p, p + 1) for s in segs for p in range(wide) if p not in ends])
    first = send(block, [(s, p, (p + 1) % wide) for s in segs if s not in late for p in ends])
    second = send(block, [(s, p, (p + run) % wide) for s in late for p in ends])
    second = send(second, [(s, p, p + 1 - run) for s in late for p in ends])
    source = jnp.where(
        lax.axis_index("section") % run > 0, 0,
        jnp.where(jnp.isin(lax.axis_index("seg"), jnp.array(late)), 2, 1),
    )
    return source.astype(jnp.int32)[None], plain, first, second


def offsets():
    return [(dz, dy, dc) for dc in (0, 1) for dy in (0, 1) for dz in (0, 3, 1, 2)]


def gather_slots(block):
    def send(part, target):
        return permute(part, "seg", target)

    below = send(block, lambda i: (i + 4) % 16)
    above = send(block, lambda i: (i - 4) % 16)
    far = send(block, lambda i: i ^ 8)
    near = jnp.stack([block, below, above, far])
    across = send(near, lambda i: i ^ 2)
    return near, across, send(near, lambda i: i ^ 1), send(across, lambda i: i ^ 1)


def gather_pairs(block):
    def send(part, target):
        return permute(part, "seg", target)

    below = send(block, lambda i: (i + 4) % 16)
    above = send(block, lambda i: (i - 4) % 16)
    far = send(block, lambda i: i ^ 8)
    mine = (block, below, above, far)
    return mine + tuple(send(part, lambda i: i ^ 1) for part in mine)


def pair_offsets():
    return [(dz, dy, dc) for dc in (0, 1) for dz in (0, 3, 1, 2) for dy in (0, 1)]


def slot_segments(me, order):
    z, y, c = me // 4, (me // 2) % 2, me % 2
    dz, dy, dc = (jnp.array(v, jnp.int32) for v in zip(*order))
    return ((z + dz) % 4) * 4 + (y ^ dy) * 2 + (c ^ dc)


def split(x):
    high = x.astype(BF16)
    return high, (x - high.astype(F32)).astype(BF16)


def dot(a, b, contract=((1,), (0,))):
    return lax.dot_general(a, b, (contract, ((), ())), preferred_element_type=F32)


def dot3(a, b):
    ah, al = a
    bh, bl = b
    return dot(ah, bh) + (dot(ah, bl) + dot(al, bh))


def phi(x):
    return jnp.where(x > 0, x, jnp.exp(jnp.minimum(x, 0.0)) - 1.0) + 1.0


def normalise(rows, gain):
    wide = rows.astype(F32)
    inverse = lax.rsqrt(jnp.mean(wide * wide, axis=-1, keepdims=True) + EPS)
    return (wide * inverse * gain.astype(F32)).astype(BF16)


def last_starts(starts_ref, count):
    lasts, last = [], jnp.int32(-1)
    for s in range(count):
        last = jnp.where(starts_ref[0, s] == 1, jnp.int32(s), last)
        lasts.append(last)
    return lasts


def norm_kernel(rows_ref, across_ref, gain_ref, out_ref):
    out_ref[0] = normalise(rows_ref[...], gain_ref[...])
    out_ref[1] = normalise(across_ref[...], gain_ref[...])


def kv_kernel(slots_ref, *refs):
    pairs, (key_ref, value_ref, gate_ref, key_out, value_out, sent_out, gate_out) = refs[:8], refs[8:]
    count = 16
    memory = jnp.concatenate([ref[...] for ref in pairs], axis=0)
    memory = memory.reshape(count * MEM, memory.shape[2])
    keys = phi(dot(memory, key_ref[...])).astype(BF16)
    values = dot(memory, value_ref[...])
    gate = jnp.broadcast_to(gate_ref[...], (8, gate_ref.shape[1]))
    rates = jax.nn.sigmoid(dot(memory, gate, ((1,), (1,))))[:, :1]
    values = rates * values
    rates = jnp.broadcast_to(rates, (count * MEM, 128))
    for slot in range(count):
        rows = pl.ds(pl.multiple_of(slots_ref[slot] * MEM, MEM), MEM)
        part = slice(slot * MEM, (slot + 1) * MEM)
        key_out[rows, :] = keys[part]
        value_out[rows, :] = values[part]
        sent_out[rows, :] = values[part].astype(BF16)
        gate_out[rows, :] = rates[part]


def solve_kernel(slots_ref, starts_ref, a_ref, b_ref, c_ref, d_ref, values_ref, rates_ref, matrix_ref, totals_ref, keys_out, writes_out, inverse_out, scaled_out):
    pieces = (a_ref, b_ref, c_ref, d_ref)
    each, rows, width = a_ref.shape
    count = 4 * each
    for slot in range(count):
        cols = pl.ds(pl.multiple_of(slots_ref[slot] * width, width), width)
        keys_out[:, cols] = pieces[slot // each][slot % each]
    keys = keys_out[...]
    gram = dot(keys, keys, ((1,), (1,)))
    probed = dot(keys, matrix_ref[...], ((1,), (1,)))
    own = lax.broadcasted_iota(jnp.int32, (rows, 1), 0) // MEM
    other = lax.broadcasted_iota(jnp.int32, (rows, rows), 1) // MEM
    last = jnp.full((rows, 1), -1, jnp.int32)
    for s, value in enumerate(last_starts(starts_ref, count)):
        last = jnp.where(own == s, value, last)
    fresh = (last < 0).astype(F32)
    masked = jnp.where((other >= last) & (other < own), gram, 0.0)
    base = jnp.sum(keys.astype(F32) * totals_ref[...], axis=-1, keepdims=True)
    scales = jnp.maximum(fresh * base + jnp.sum(masked, axis=-1, keepdims=True), 1.0)
    rates = rates_ref[:, :1]
    weights = fresh * rates / scales
    same = lax.broadcasted_iota(jnp.int32, (rows, rows), 0) == lax.broadcasted_iota(jnp.int32, (rows, rows), 1)
    current = jnp.concatenate(
        [values_ref[...] - weights * probed, same.astype(F32), jnp.where(same, weights, 0.0)], axis=1
    )
    power = split(masked * (rates / scales))
    current = current - dot3(power, split(current))
    for _ in range(3):
        power = split(dot3(power, power))
        current = current + dot3(power, split(current))
    wide = current.shape[1] - 2 * rows
    writes_out[...] = current[:, :wide]
    for out, part in ((inverse_out, current[:, wide : wide + rows]), (scaled_out, current[:, wide + rows :])):
        out[...] = part.astype(BF16)


def next_kernel(starts_ref, keys_ref, writes_ref, matrix_ref, totals_ref, matrix_out, totals_out):
    rows = keys_ref.shape[0]
    last = last_starts(starts_ref, rows // MEM)[-1]
    fresh = (last < 0).astype(F32)
    keys = keys_ref[...]
    own = lax.broadcasted_iota(jnp.int32, (rows, 1), 0) // MEM
    writes = jnp.where(own >= last, writes_ref[...], 0.0)
    added = dot(writes.astype(BF16), keys, ((0,), (0,)))
    matrix_out[...] = (fresh * matrix_ref[...].astype(F32) + added).astype(BF16)
    seen = lax.broadcasted_iota(jnp.int32, (8, rows), 1) // MEM >= last
    sums = dot(seen.astype(F32).astype(BF16), keys)[:1]
    totals_out[...] = fresh * totals_ref[...] + sums


def query_kernel(source_ref, first_ref, second_ref, third_ref, gain_ref, weight_ref, out_ref, rows_ref, normed_ref, landed):
    @pl.when(pl.program_id(0) == 0)
    def _():
        for number, ref in enumerate((first_ref, second_ref, third_ref)):

            @pl.when(source_ref[0] == number)
            def _(ref=ref):
                copy = pltpu.make_async_copy(ref, rows_ref, landed)
                copy.start()
                copy.wait()

        normed_ref[...] = normalise(rows_ref[...], gain_ref[...])

    out_ref[...] = phi(dot(normed_ref[...], weight_ref[...])).astype(BF16)


def similarity_kernel(me_ref, starts_ref, queries_ref, keys_ref, totals_ref, inverse_ref, scaled_ref, probe_out, mix_out, scale_out):
    rows = keys_ref.shape[0]
    me = me_ref[0]
    last = jnp.int32(-1)
    for s, value in enumerate(last_starts(starts_ref, rows // MEM)):
        last = jnp.where(me == s, value, last)
    fresh = (last < 0).astype(F32)
    queries = queries_ref[...]
    wide = queries.astype(F32)
    other = lax.broadcasted_iota(jnp.int32, (1, rows), 1) // MEM
    masked = jnp.where((other >= last) & (other < me), dot(queries, keys_ref[...], ((1,), (1,))), 0.0)
    base = jnp.sum(wide * totals_ref[...], axis=-1, keepdims=True)
    inverse = 1.0 / jnp.maximum(fresh * base + jnp.sum(masked, axis=-1, keepdims=True), 1.0)
    masked = masked.astype(BF16)
    mix_out[...] = dot(masked, inverse_ref[...]).astype(BF16)
    probed = dot(dot(masked, scaled_ref[...]).astype(BF16), keys_ref[...])
    probe_out[...] = (fresh * wide - probed).astype(BF16)
    scale_out[...] = jnp.broadcast_to(inverse, scale_out.shape)


def near_copies(z, place_ref, held_ref, arrived, matrix_ref):
    wide = held_ref.shape[1]
    return [pltpu.make_async_copy(matrix_ref.at[pl.ds(z * wide, wide)], held_ref.at[z], arrived.at[z, 0])]


def away_copies(z, place_ref, held_ref, arrived, matrix_ref, bulk_ref):
    few = bulk_ref.shape[1]
    width = held_ref.shape[1] // 2
    many = width - few
    return [
        pltpu.make_async_copy(source, held_ref.at[z, pl.ds(start, size)], arrived.at[z, number])
        for number, (source, start, size) in enumerate(
            (
                (matrix_ref.at[pl.ds(2 * z * many, many)], 0, many),
                (bulk_ref.at[2 * z], many, few),
                (matrix_ref.at[pl.ds((2 * z + 1) * many, many)], width, many),
                (bulk_ref.at[2 * z + 1], width + many, few),
            )
        )
    ]


def read_kernel(copies, parts, place_ref, probe_ref, mix_ref, scale_ref, rows_ref, mine_ref, theirs_ref, *rest):
    matrix_refs, (out_ref, held_ref, arrived) = rest[:parts], rest[-3:]
    step = pl.program_id(0)

    @pl.when(step == 0)
    def _():
        for z in range(4):
            for copy in copies(z, place_ref, held_ref, arrived, *matrix_refs):
                copy.start()

    for copy in copies(step, place_ref, held_ref, arrived, *matrix_refs):
        copy.wait()
    width = mine_ref.shape[2]
    base = dot(probe_ref[...], held_ref[step], ((1,), (1,)))
    scale = scale_ref[:, :1]
    swap = place_ref[1] == 1
    for side in range(2):
        cols = slice(side * width, (side + 1) * width)
        writes = jnp.where(swap == (side == 0), theirs_ref[0], mine_ref[0])
        low = dot(mix_ref[...], writes)
        out_ref[:, cols] = (rows_ref[:, cols].astype(F32) + scale * (base[:, cols] + low)).astype(BF16)


def read_half(half, me, probe, mix, scale, entering, values, matrices, copies, previous=None):
    count, depth = probe.shape
    rows, width = values[0].shape[1:]
    distance = (jnp.arange(4, dtype=jnp.int32) - me // 4) % 4
    slot_of = jnp.where(distance == 3, 1, jnp.where(distance == 0, 0, distance + 1))
    place = jnp.concatenate([jnp.stack([half, me % 2]), slot_of])
    args = [place, probe, mix, scale, entering, *values, *matrices]
    specs = [
        pl.BlockSpec((count, depth), lambda z, p: (0, 0)),
        pl.BlockSpec((count, rows), lambda z, p: (0, 0)),
        pl.BlockSpec((count, 128), lambda z, p: (0, 0)),
        pl.BlockSpec((count, 2 * width), lambda z, p: (0, 2 * z + p[0])),
        pl.BlockSpec((1, rows, width), lambda z, p: (p[2 + z], 0, 0)),
        pl.BlockSpec((1, rows, width), lambda z, p: (p[2 + z], 0, 0)),
    ] + [pl.BlockSpec(memory_space=pl.ANY)] * len(matrices)
    if previous is not None:
        args.append(previous)
        specs.append(pl.BlockSpec(memory_space=pl.ANY))
    return pl.pallas_call(
        functools.partial(read_kernel, copies, len(matrices)),
        out_shape=shape(entering.shape, BF16),
        grid_spec=pltpu.PrefetchScalarGridSpec(
            num_scalar_prefetch=1,
            grid=(4,),
            in_specs=specs,
            out_specs=pl.BlockSpec((count, 2 * width), lambda z, p: (0, 2 * z + p[0])),
            scratch_shapes=[pltpu.VMEM((4, 2 * width, depth), BF16), pltpu.SemaphoreType.DMA((4, 4))],
        ),
        input_output_aliases={} if previous is None else {len(args) - 1: 0},
        interpret=INTERPRET,
    )(*args)


def call(kernel, outs, *args, specs, scratch=()):
    return pl.pallas_call(
        kernel, out_shape=outs, in_specs=list(specs),
        out_specs=jax.tree.map(lambda _: VM, outs), scratch_shapes=scratch, interpret=INTERPRET,
    )(*args)


def shape(dims, kind):
    return jax.ShapeDtypeStruct(dims, kind)


def local(leaving, w_query, w_key, w_value, w_gate, norm_gain, memory_matrix, key_totals, doc_starts):
    me = lax.axis_index("seg").astype(jnp.int32)
    slots = slot_segments(me, offsets())
    pair_slots = slot_segments(me, pair_offsets())
    mine = jnp.full((1,), me)
    leaving, matrix = leaving[0, 0], memory_matrix[0]
    width, features, depth = matrix.shape[0], leaving.shape[1], matrix.shape[1]
    rows = 16 * MEM
    head = shifted(leaving[:MEM])
    across = shifted_across(leaving[:MEM])
    entering = shifted_rows(leaving)
    groups = [[i for i in range(16) if (i // 2) % 2 == y] for y in (0, 1)]
    near = lax.all_gather(matrix, "seg", axis=0, tiled=True, axis_index_groups=groups)
    trimmed = matrix[: 7 * width // 8]
    partner = permute(trimmed, "seg", lambda i: i ^ 2)
    away = lax.all_gather(partner, "seg", axis=0, tiled=True, axis_index_groups=groups)
    bulk = near.reshape(8, width, depth)[:, 7 * width // 8 :]
    bulk = permute(bulk, "seg", lambda i: i ^ 2)

    normed = call(
        norm_kernel, shape((2, MEM, features), BF16), head, across, norm_gain, specs=[VM] * 3
    )
    memory = gather_pairs(normed)
    key_part, values, sent, rates = call(
        kv_kernel,
        (
            shape((rows, w_key.shape[2]), BF16),
            shape((rows, width), F32),
            shape((rows, width), BF16),
            shape((rows, 128), F32),
        ),
        pair_slots, *memory, w_key[0], w_value[0], w_gate,
        specs=[SM] + [VM] * 11,
    )
    pieces = gather_slots(key_part)
    value_slots = gather_slots(sent)
    keys, writes, inverse, scaled = call(
        solve_kernel,
        (shape((rows, depth), BF16), shape((rows, width), F32), shape((rows, rows), BF16), shape((rows, rows), BF16)),
        slots, doc_starts, *pieces, values, rates, matrix, key_totals,
        specs=[SM, SM] + [VM] * 8,
    )
    matrix_next, totals_next = call(
        next_kernel,
        (shape((width, depth), BF16), shape((1, depth), F32)),
        doc_starts, keys, writes, matrix, key_totals,
        specs=[SM] + [VM] * 4,
    )

    count = leaving.shape[0]
    any_space = pl.BlockSpec(memory_space=pl.ANY)
    block = depth // 4
    queries, entering = pl.pallas_call(
        query_kernel,
        out_shape=(shape((count, depth), BF16), shape((count, features), BF16)),
        grid=(4,),
        in_specs=[SM]
        + [any_space] * 3
        + [
            pl.BlockSpec((1, features), lambda j: (0, 0)),
            pl.BlockSpec((features, block), lambda j: (0, j)),
        ],
        out_specs=(pl.BlockSpec((count, block), lambda j: (0, j)), pl.BlockSpec((count, features), lambda j: (0, 0))),
        scratch_shapes=[pltpu.VMEM((count, features), BF16), pltpu.SemaphoreType.DMA],
        interpret=INTERPRET,
    )(*entering, norm_gain, w_query[0])
    probe, mix, scale = call(
        similarity_kernel,
        (
            shape((count, depth), BF16),
            shape((count, rows), BF16),
            shape((count, 128), F32),
        ),
        mine, doc_starts, queries, keys, key_totals, inverse, scaled,
        specs=[SM, SM] + [VM] * 5,
    )
    half = (me // 2) % 2
    parts = (me, probe, mix, scale, entering)
    updated = read_half(half, *parts, value_slots[0::2], (near,), near_copies)
    updated = read_half(1 - half, *parts, value_slots[1::2], (away, bulk), away_copies, updated)
    return updated[None, None], matrix_next[None], totals_next


def solution(mesh):
    return jax.shard_map(
        local,
        mesh=mesh,
        in_specs=(
            P("seg", "section", None, None),
            P("section", None, None),
            P("section", None, "seg"),
            P("section", None, "seg"),
            P("section", None),
            P("section", None),
            P("section", "seg", None),
            P("section", None),
            P("section", None),
        ),
        out_specs=(P("seg", "section", None, None), P("section", "seg", None), P("section", None)),
        check_vma=False,
    )
```

```python
import functools

import jax
import jax.numpy as jnp
from jax import lax
from jax.experimental import pallas as pl
from jax.experimental.pallas import tpu as pltpu
from jax.sharding import PartitionSpec as P


MEM = 16
EPS = 1e-05
INTERPRET = False
F32 = jnp.float32
BF16 = jnp.bfloat16


VM = pl.BlockSpec(memory_space=pltpu.VMEM)
SM = pl.BlockSpec(memory_space=pltpu.SMEM)


def permute(block, axis, target):
    size = lax.axis_size(axis)
    return lax.ppermute(block, axis, [(i, target(i)) for i in range(size)])


def shifted(block):
    return permute(block, "section", lambda i: (i + 1) % lax.axis_size("section"))


def shifted_across(block):
    wide = lax.axis_size("section")
    pairs = [
        (s * wide + p, (s ^ 2) * wide + (p + 1) % wide)
        for s in range(lax.axis_size("seg"))
        for p in range(wide)
    ]
    return lax.ppermute(block, ("seg", "section"), pairs)


def shifted_rows(block):
    wide, run = lax.axis_size("section"), lax.axis_size("section") // 2
    ends = [p for p in range(wide) if p % run == run - 1]
    segs = range(lax.axis_size("seg"))
    late = [s for s in segs if (s ^ (s // 2)) % 2]

    def send(part, pairs):
        return lax.ppermute(part, ("seg", "section"), [(s * wide + p, s * wide + q) for s, p, q in pairs])

    plain = send(block, [(s, p, p + 1) for s in segs for p in range(wide) if p not in ends])
    first = send(block, [(s, p, (p + 1) % wide) for s in segs if s not in late for p in ends])
    second = send(block, [(s, p, (p + run) % wide) for s in late for p in ends])
    second = send(second, [(s, p, p + 1 - run) for s in late for p in ends])
    me = lax.axis_index("seg")
    source = jnp.where(lax.axis_index("section") % run > 0, 0, 1 + (me + me // 2) % 2)
    return source.astype(jnp.int32)[None], plain, first, second


def offsets():
    return [(dz, dy, dc) for dc in (0, 1) for dy in (0, 1) for dz in (0, 3, 1, 2)]


def gather_slots(block):
    def send(part, target):
        return permute(part, "seg", target)

    below = send(block, lambda i: (i + 4) % 16)
    above = send(block, lambda i: (i - 4) % 16)
    far = send(block, lambda i: i ^ 8)
    near = jnp.stack([block, below, above, far])
    across = send(near, lambda i: i ^ 2)
    return near, across, send(near, lambda i: i ^ 1), send(across, lambda i: i ^ 1)


def gather_pairs(block):
    def send(part, target):
        return permute(part, "seg", target)

    below = send(block, lambda i: (i + 4) % 16)
    above = send(block, lambda i: (i - 4) % 16)
    far = send(block, lambda i: i ^ 8)
    mine = (block, below, above, far)
    return mine + tuple(send(part, lambda i: i ^ 1) for part in mine)


def pair_offsets():
    return [(dz, dy, dc) for dc in (0, 1) for dz in (0, 3, 1, 2) for dy in (0, 1)]


def slot_segment(me, offset):
    z, y, c = me // 4, (me // 2) % 2, me % 2
    dz, dy, dc = offset
    return ((z + dz) % 4) * 4 + ((y + dy) % 2) * 2 + (c + dc) % 2


def split(x):
    high = x.astype(BF16)
    return high, (x - high.astype(F32)).astype(BF16)


def dot(a, b, contract=((1,), (0,))):
    return lax.dot_general(a, b, (contract, ((), ())), preferred_element_type=F32)


def dot3(a, b):
    ah, al = a
    bh, bl = b
    return dot(ah, bh) + (dot(ah, bl) + dot(al, bh))


def phi(x):
    return jnp.where(x > 0, x, jnp.exp(jnp.minimum(x, 0.0)) - 1.0) + 1.0


def normalise(rows, gain):
    wide = rows.astype(F32)
    inverse = lax.rsqrt(jnp.mean(wide * wide, axis=-1, keepdims=True) + EPS)
    return (wide * inverse * gain.astype(F32)).astype(BF16)


def last_starts(starts_ref, count):
    lasts, last = [], jnp.int32(-1)
    for s in range(count):
        last = jnp.where(starts_ref[0, s] == 1, jnp.int32(s), last)
        lasts.append(last)
    return lasts


def norm_kernel(rows_ref, across_ref, gain_ref, out_ref):
    out_ref[0] = normalise(rows_ref[...], gain_ref[...])
    out_ref[1] = normalise(across_ref[...], gain_ref[...])


def kv_kernel(me_ref, *refs):
    pairs, (key_ref, value_ref, gate_ref, key_out, value_out, sent_out, gate_out) = refs[:8], refs[8:]
    count = 16
    memory = jnp.concatenate([ref[...] for ref in pairs], axis=0)
    memory = memory.reshape(count * MEM, memory.shape[2])
    keys = phi(dot(memory, key_ref[...])).astype(BF16)
    values = dot(memory, value_ref[...])
    gate = jnp.broadcast_to(gate_ref[...], (8, gate_ref.shape[1]))
    rates = jax.nn.sigmoid(dot(memory, gate, ((1,), (1,))))[:, :1]
    values = rates * values
    rates = jnp.broadcast_to(rates, (count * MEM, 128))
    for slot, offset in enumerate(pair_offsets()):
        rows = pl.ds(pl.multiple_of(slot_segment(me_ref[0], offset) * MEM, MEM), MEM)
        part = slice(slot * MEM, (slot + 1) * MEM)
        key_out[rows, :] = keys[part]
        value_out[rows, :] = values[part]
        sent_out[rows, :] = values[part].astype(BF16)
        gate_out[rows, :] = rates[part]


def solve_kernel(me_ref, starts_ref, a_ref, b_ref, c_ref, d_ref, values_ref, rates_ref, matrix_ref, totals_ref, keys_out, writes_out, inverse_out, scaled_out):
    pieces = (a_ref, b_ref, c_ref, d_ref)
    each, rows, width = a_ref.shape
    count = 4 * each
    for slot, offset in enumerate(offsets()):
        cols = pl.ds(pl.multiple_of(slot_segment(me_ref[0], offset) * width, width), width)
        keys_out[:, cols] = pieces[slot // each][slot % each]
    keys = keys_out[...]
    gram = dot(keys, keys, ((1,), (1,)))
    probed = dot(keys, matrix_ref[...], ((1,), (1,)))
    own = lax.broadcasted_iota(jnp.int32, (rows, 1), 0) // MEM
    other = lax.broadcasted_iota(jnp.int32, (rows, rows), 1) // MEM
    last = jnp.full((rows, 1), -1, jnp.int32)
    for s, value in enumerate(last_starts(starts_ref, count)):
        last = jnp.where(own == s, value, last)
    fresh = (last < 0).astype(F32)
    masked = jnp.where((other >= last) & (other < own), gram, 0.0)
    base = jnp.sum(keys.astype(F32) * totals_ref[...], axis=-1, keepdims=True)
    scales = jnp.maximum(fresh * base + jnp.sum(masked, axis=-1, keepdims=True), 1.0)
    rates = rates_ref[:, :1]
    weights = fresh * rates / scales
    same = lax.broadcasted_iota(jnp.int32, (rows, rows), 0) == lax.broadcasted_iota(jnp.int32, (rows, rows), 1)
    current = jnp.concatenate([values_ref[...] - weights * probed, same.astype(F32)], axis=1)
    power = split(masked * (rates / scales))
    current = current - dot3(power, split(current))
    for _ in range(3):
        power = split(dot3(power, power))
        current = current + dot3(power, split(current))
    wide = current.shape[1] - rows
    writes_out[...] = current[:, :wide]
    inverse = current[:, wide:]
    inverse_out[...] = inverse.astype(BF16)
    scaled_out[...] = (inverse * jnp.sum(jnp.where(same, weights, 0.0), axis=0, keepdims=True)).astype(BF16)


def next_kernel(starts_ref, keys_ref, writes_ref, matrix_ref, totals_ref, matrix_out, totals_out):
    rows = keys_ref.shape[0]
    last = last_starts(starts_ref, rows // MEM)[-1]
    fresh = (last < 0).astype(F32)
    keys = keys_ref[...]
    own = lax.broadcasted_iota(jnp.int32, (rows, 1), 0) // MEM
    writes = jnp.where(own >= last, writes_ref[...], 0.0)
    added = dot(writes.astype(BF16), keys, ((0,), (0,)))
    matrix_out[...] = (fresh * matrix_ref[...].astype(F32) + added).astype(BF16)
    seen = lax.broadcasted_iota(jnp.int32, (8, rows), 1) // MEM >= last
    sums = dot(seen.astype(F32).astype(BF16), keys)[:1]
    totals_out[...] = fresh * totals_ref[...] + sums


def query_kernel(source_ref, first_ref, second_ref, third_ref, gain_ref, weight_ref, out_ref, rows_ref, normed_ref, landed):
    @pl.when(pl.program_id(0) == 0)
    def _():
        for number, ref in enumerate((first_ref, second_ref, third_ref)):

            @pl.when(source_ref[0] == number)
            def _(ref=ref):
                copy = pltpu.make_async_copy(ref, rows_ref, landed)
                copy.start()
                copy.wait()

        normed_ref[...] = normalise(rows_ref[...], gain_ref[...])

    out_ref[...] = phi(dot(normed_ref[...], weight_ref[...])).astype(BF16)


def similarity_kernel(me_ref, starts_ref, queries_ref, keys_ref, totals_ref, inverse_ref, scaled_ref, probe_out, mix_out, scale_out):
    rows = keys_ref.shape[0]
    me = me_ref[0]
    last = jnp.int32(-1)
    for s, value in enumerate(last_starts(starts_ref, rows // MEM)):
        last = jnp.where(me == s, value, last)
    fresh = (last < 0).astype(F32)
    queries = queries_ref[...]
    wide = queries.astype(F32)
    other = lax.broadcasted_iota(jnp.int32, (1, rows), 1) // MEM
    masked = jnp.where((other >= last) & (other < me), dot(queries, keys_ref[...], ((1,), (1,))), 0.0)
    base = jnp.sum(wide * totals_ref[...], axis=-1, keepdims=True)
    inverse = 1.0 / jnp.maximum(fresh * base + jnp.sum(masked, axis=-1, keepdims=True), 1.0)
    masked = masked.astype(BF16)
    mix_out[...] = dot(masked, inverse_ref[...]).astype(BF16)
    probed = dot(dot(masked, scaled_ref[...]).astype(BF16), keys_ref[...])
    probe_out[...] = (fresh * wide - probed).astype(BF16)
    scale_out[...] = jnp.broadcast_to(inverse, scale_out.shape)


def near_copies(z, place_ref, held_ref, arrived, matrix_ref):
    wide = held_ref.shape[1]
    return [pltpu.make_async_copy(matrix_ref.at[pl.ds(z * wide, wide)], held_ref.at[z], arrived.at[z, 0])]


def away_copies(z, place_ref, held_ref, arrived, matrix_ref, mine_ref, theirs_ref):
    few = mine_ref.shape[1]
    width = held_ref.shape[1] // 2
    many = width - few
    core = place_ref[0] % 2
    return [
        pltpu.make_async_copy(source, held_ref.at[z, pl.ds(start, size)], arrived.at[z, number])
        for number, (source, start, size) in enumerate(
            (
                (matrix_ref.at[pl.ds(2 * z * many, many)], 0, many),
                (matrix_ref.at[pl.ds((2 * z + 1) * many, many)], width, many),
                (mine_ref.at[z], pl.multiple_of(core * width + many, few), few),
                (theirs_ref.at[z], pl.multiple_of((1 - core) * width + many, few), few),
            )
        )
    ]


def read_kernel(copies, parts, place_ref, probe_ref, mix_ref, scale_ref, rows_ref, mine_ref, theirs_ref, *rest):
    matrix_refs, (out_ref, held_ref, arrived) = rest[:parts], rest[-3:]
    step = pl.program_id(0)

    @pl.when(step == 0)
    def _():
        for z in range(4):
            for copy in copies(z, place_ref, held_ref, arrived, *matrix_refs):
                copy.start()

    for copy in copies(step, place_ref, held_ref, arrived, *matrix_refs):
        copy.wait()
    width = mine_ref.shape[2]
    base = dot(probe_ref[...], held_ref[step], ((1,), (1,)))
    scale = scale_ref[:, :1]
    swap = place_ref[0] % 2 == 1
    for side in range(2):
        cols = slice(side * width, (side + 1) * width)
        writes = jnp.where(swap == (side == 0), theirs_ref[0], mine_ref[0])
        low = dot(mix_ref[...], writes)
        out_ref[:, cols] = (rows_ref[:, cols].astype(F32) + scale * (base[:, cols] + low)).astype(BF16)


def read_half(half, me, probe, mix, scale, entering, values, matrices, copies, previous=None):
    count, depth = probe.shape
    rows, width = values[0].shape[1:]

    def half_of(place):
        return (place[0] // 2 + half) % 2

    def slot_of(z, place):
        distance = (z + 4 - place[0] // 4) % 4
        return jnp.where(distance == 3, 1, jnp.where(distance == 0, 0, distance + 1))

    args = [me, probe, mix, scale, entering, *values, *matrices]
    specs = [
        pl.BlockSpec((count, depth), lambda z, p: (0, 0)),
        pl.BlockSpec((count, rows), lambda z, p: (0, 0)),
        pl.BlockSpec((count, 128), lambda z, p: (0, 0)),
        pl.BlockSpec((count, 2 * width), lambda z, p: (0, 2 * z + half_of(p))),
        pl.BlockSpec((1, rows, width), lambda z, p: (slot_of(z, p), 0, 0)),
        pl.BlockSpec((1, rows, width), lambda z, p: (slot_of(z, p), 0, 0)),
    ] + [pl.BlockSpec(memory_space=pl.ANY)] * len(matrices)
    if previous is not None:
        args.append(previous)
        specs.append(pl.BlockSpec(memory_space=pl.ANY))
    return pl.pallas_call(
        functools.partial(read_kernel, copies, len(matrices)),
        out_shape=shape(entering.shape, BF16),
        grid_spec=pltpu.PrefetchScalarGridSpec(
            num_scalar_prefetch=1,
            grid=(4,),
            in_specs=specs,
            out_specs=pl.BlockSpec((count, 2 * width), lambda z, p: (0, 2 * z + half_of(p))),
            scratch_shapes=[pltpu.VMEM((4, 2 * width, depth), BF16), pltpu.SemaphoreType.DMA((4, 4))],
        ),
        input_output_aliases={} if previous is None else {len(args) - 1: 0},
        interpret=INTERPRET,
    )(*args)


def call(kernel, outs, *args, specs, scratch=()):
    return pl.pallas_call(
        kernel, out_shape=outs, in_specs=list(specs),
        out_specs=jax.tree.map(lambda _: VM, outs), scratch_shapes=scratch, interpret=INTERPRET,
    )(*args)


def shape(dims, kind):
    return jax.ShapeDtypeStruct(dims, kind)


def local(leaving, w_query, w_key, w_value, w_gate, norm_gain, memory_matrix, key_totals, doc_starts):
    me = lax.axis_index("seg").astype(jnp.int32)
    mine = jnp.full((1,), me)
    leaving, matrix = leaving[0, 0], memory_matrix[0]
    width, features, depth = matrix.shape[0], leaving.shape[1], matrix.shape[1]
    rows = 16 * MEM
    head = shifted(leaving[:MEM])
    across = shifted_across(leaving[:MEM])
    entering = shifted_rows(leaving)
    groups = [[i for i in range(16) if (i // 2) % 2 == y] for y in (0, 1)]
    near = lax.all_gather(matrix, "seg", axis=0, tiled=True, axis_index_groups=groups)
    trimmed = matrix[: 3 * width // 4]
    partner = permute(trimmed, "seg", lambda i: i ^ 2)
    away = lax.all_gather(partner, "seg", axis=0, tiled=True, axis_index_groups=groups)
    bulk = lax.dynamic_slice(
        near.reshape(4, 2, width, depth), (0, me % 2, 3 * width // 4, 0), (4, 1, width // 4, depth)
    )[:, 0]
    bulk = permute(bulk, "seg", lambda i: i ^ 2)
    twin = permute(bulk, "seg", lambda i: i ^ 1)

    normed = call(
        norm_kernel, shape((2, MEM, features), BF16), head, across, norm_gain, specs=[VM] * 3
    )
    memory = gather_pairs(normed)
    key_part, values, sent, rates = call(
        kv_kernel,
        (
            shape((rows, w_key.shape[2]), BF16),
            shape((rows, width), F32),
            shape((rows, width), BF16),
            shape((rows, 128), F32),
        ),
        mine, *memory, w_key[0], w_value[0], w_gate,
        specs=[SM] + [VM] * 11,
    )
    pieces = gather_slots(key_part)
    value_slots = gather_slots(sent)
    keys, writes, inverse, scaled = call(
        solve_kernel,
        (shape((rows, depth), BF16), shape((rows, width), F32), shape((rows, rows), BF16), shape((rows, rows), BF16)),
        mine, doc_starts, *pieces, values, rates, matrix, key_totals,
        specs=[SM, SM] + [VM] * 8,
    )
    matrix_next, totals_next = call(
        next_kernel,
        (shape((width, depth), BF16), shape((1, depth), F32)),
        doc_starts, keys, writes, matrix, key_totals,
        specs=[SM] + [VM] * 4,
    )

    count = leaving.shape[0]
    any_space = pl.BlockSpec(memory_space=pl.ANY if INTERPRET else pltpu.HBM)
    block = depth // 4
    queries, entering = pl.pallas_call(
        query_kernel,
        out_shape=(shape((count, depth), BF16), shape((count, features), BF16)),
        grid=(4,),
        in_specs=[SM]
        + [any_space] * 3
        + [
            pl.BlockSpec((1, features), lambda j: (0, 0)),
            pl.BlockSpec((features, block), lambda j: (0, j)),
        ],
        out_specs=(pl.BlockSpec((count, block), lambda j: (0, j)), pl.BlockSpec((count, features), lambda j: (0, 0))),
        scratch_shapes=[pltpu.VMEM((count, features), BF16), pltpu.SemaphoreType.DMA],
        interpret=INTERPRET,
    )(*entering, norm_gain, w_query[0])
    probe, mix, scale = call(
        similarity_kernel,
        (
            shape((count, depth), BF16),
            shape((count, rows), BF16),
            shape((count, 128), F32),
        ),
        mine, doc_starts, queries, keys, key_totals, inverse, scaled,
        specs=[SM, SM] + [VM] * 5,
    )
    parts = (mine, probe, mix, scale, entering)
    updated = read_half(0, *parts, value_slots[0::2], (near,), near_copies)
    updated = read_half(1, *parts, value_slots[1::2], (away, bulk, twin), away_copies, updated)
    return updated[None, None], matrix_next[None], totals_next


def solution(mesh):
    return jax.shard_map(
        local,
        mesh=mesh,
        in_specs=(
            P("seg", "section", None, None),
            P("section", None, None),
            P("section", None, "seg"),
            P("section", None, "seg"),
            P("section", None),
            P("section", None),
            P("section", "seg", None),
            P("section", None),
            P("section", None),
        ),
        out_specs=(P("seg", "section", None, None), P("section", "seg", None), P("section", None)),
        check_vma=False,
    )
```
